256 devices in a mesh: row: 16 (over x_hi, y, core), col: 16 (over x_lo, z).
Axes of the slice: x: 4 (x_hi: 2, x_lo: 2; x = x_hi * 2 + x_lo), y: 4, z: 8, core: 2. Of those that a mesh axis runs over, the one named last changes fastest.
Arguments:
- video_rows: bfloat16 [98304, 1024], P(('row', 'col')), may hold values from -1.5 to 1.5
- video_ids: int32 [98304], P(('row', 'col')), may hold values from 0 to 767
- imu_rows: bfloat16 [98304, 1024], P(('row', 'col')), may hold values from -1.5 to 1.5
- imu_ids: int32 [98304], P(('row', 'col')), may hold values from 0 to 767
- audio_rows: bfloat16 [98304, 1024], P(('row', 'col')), may hold values from -1.5 to 1.5
- audio_ids: int32 [98304], P(('row', 'col')), may hold values from 0 to 767
- imu_log_scale: float32 [1], replicated, may hold values from 0 to 1
- imu_bias: float32 [1], replicated, may hold values from -3 to -1
- audio_log_scale: float32 [1], replicated, may hold values from 0 to 1
- audio_bias: float32 [1], replicated, may hold values from -3 to -1
Outputs:
- video_grad: float32 [98304, 1024], P(('row', 'col'))
- imu_grad: float32 [98304, 1024], P(('row', 'col'))
- audio_grad: float32 [98304, 1024], P(('row', 'col'))
- row_loss: float32 [98304], P(('row', 'col'))
The draws below stay inside these ranges and needn't reach their ends.
All inputs are finite; a program needn't handle non-finite values.
Results may differ from the reference program's by a relative error of at most 0.0025.
Values may be sent and summed in bfloat16 or wider, within the bound.
A program may use at most 128 MiB of HBM per device.

```python
import jax
import jax.numpy as jnp
from jax import lax

D = 1024
TOK_DEV = 384
STEPS = 4
BATCH = 98304
IDS = 768
N_ROW = 16
N_COL = 16


def place_ends(values, rng, least, top_value):
    longest = values.shape.index(max(values.shape))
    spots = []
    for shift in (0, 1):
        where = [jax.random.randint(jax.random.fold_in(rng, axis), (), 0, length) for axis, length in enumerate(values.shape)]
        where[longest] = (where[longest] + shift) % values.shape[longest]
        spots.append(tuple(where))
    return values.at[spots[0]].set(least).at[spots[1]].set(top_value)


def block_scale(own_key, shape, cuts, low, high):
    gain, own = 1.0, jax.random.fold_in(own_key, 6)
    for position, shards_of in cuts:
        heights = jnp.exp(jax.random.uniform(jax.random.fold_in(own, position), (shards_of,), jnp.float32, low / len(cuts), high / len(cuts)))
        gain = gain * jnp.repeat(heights, shape[position] // shards_of).reshape([-1 if axis == position else 1 for axis in range(len(shape))])
    return gain


def normal_values(key, dims, scale, limit, shards=(), kind=jnp.bfloat16):
    array = jax.random.normal(key, dims, jnp.float32) * scale
    if len(shards) > 0:
        array = block_scale(key, dims, shards, -0.22, 0.18) * array
    return jnp.clip(array, min=-limit, max=limit).astype(kind)


def setup_inputs(seed: int = 0) -> dict:
    keys = jax.random.split(jax.random.key(seed), 11)
    video_rows = normal_values(keys[0], (BATCH, D), 0.25, 1.5, ((0, 256),))
    video_ids = place_ends(jax.random.randint(keys[1], (BATCH,), 0, IDS), jax.random.fold_in(keys[1], 1), 0, IDS - 1).astype(jnp.int32)
    imu_rows = normal_values(keys[2], (BATCH, D), 0.25, 1.5, ((0, 256),))
    imu_ids = place_ends(jax.random.randint(keys[3], (BATCH,), 0, IDS), jax.random.fold_in(keys[3], 1), 0, IDS - 1).astype(jnp.int32)
    audio_rows = normal_values(keys[4], (BATCH, D), 0.25, 1.5, ((0, 256),))
    audio_ids = place_ends(jax.random.randint(keys[5], (BATCH,), 0, IDS), jax.random.fold_in(keys[5], 1), 0, IDS - 1).astype(jnp.int32)
    imu_log_scale = jnp.clip(jax.random.uniform(keys[6], (1,), jnp.float32, 0.0, 1.0), 0.0, 1.0)
    imu_bias = jnp.clip(jax.random.uniform(keys[7], (1,), jnp.float32, -3.0, -1.0), -3.0, -1.0)
    audio_log_scale = jnp.clip(jax.random.uniform(keys[8], (1,), jnp.float32, 0.0, 1.0), 0.0, 1.0)
    audio_bias = jnp.clip(jax.random.uniform(keys[9], (1,), jnp.float32, -3.0, -1.0), -3.0, -1.0)
    return {"video_rows": video_rows, "video_ids": video_ids, "imu_rows": imu_rows, "imu_ids": imu_ids, "audio_rows": audio_rows, "audio_ids": audio_ids, "imu_log_scale": imu_log_scale, "imu_bias": imu_bias, "audio_log_scale": audio_log_scale, "audio_bias": audio_bias}


def pair_tile(video_block, video_tags, partner, partner_tags, scale, offset):
    products = lax.dot_general(video_block, partner, (((1,), (1,)), ((), ())), preferred_element_type=jnp.float32)
    logits = scale * products + offset
    signs = jnp.where(video_tags[:, None] == partner_tags[None, :], 1.0, -1.0).astype(logits.dtype)
    losses = jax.nn.softplus(-signs * logits)
    weighted = (-signs * jax.nn.sigmoid(-signs * logits) * scale).astype(jnp.bfloat16)
    video_term = jnp.dot(weighted, partner, preferred_element_type=jnp.float32)
    partner_term = lax.dot_general(weighted, video_block, (((0,), (0,)), ((), ())), preferred_element_type=jnp.float32)
    return jnp.sum(losses, axis=1), video_term, partner_term


def reference(video_rows, video_ids, imu_rows, imu_ids, audio_rows, audio_ids, imu_log_scale, imu_bias, audio_log_scale, audio_bias):
    blocks = N_ROW * N_COL
    shape_four = (N_ROW, N_COL, TOK_DEV, D)
    shape_tags = (N_ROW, N_COL, TOK_DEV)
    video_flat = video_rows.reshape(blocks, TOK_DEV, D)
    video_tags = video_ids.reshape(blocks, TOK_DEV)
    imu_four = imu_rows.reshape(shape_four)
    imu_tags = imu_ids.reshape(shape_tags)
    audio_four = audio_rows.reshape(shape_four)
    audio_tags = audio_ids.reshape(shape_tags)
    scale_imu = jnp.exp(imu_log_scale[0])
    scale_audio = jnp.exp(audio_log_scale[0])
    offset_imu = imu_bias[0]
    offset_audio = audio_bias[0]
    loss_sum = jnp.zeros((blocks, TOK_DEV), jnp.float32)
    video_acc = jnp.zeros((blocks, TOK_DEV, D), jnp.float32)
    imu_acc = jnp.zeros(shape_four, jnp.float32)
    audio_acc = jnp.zeros(shape_four, jnp.float32)
    for rotation in range(STEPS):
        imu_now = jnp.roll(imu_four, rotation, axis=0).reshape(blocks, TOK_DEV, D)
        imu_tag_now = jnp.roll(imu_tags, rotation, axis=0).reshape(blocks, TOK_DEV)
        audio_now = jnp.roll(audio_four, rotation, axis=1).reshape(blocks, TOK_DEV, D)
        audio_tag_now = jnp.roll(audio_tags, rotation, axis=1).reshape(blocks, TOK_DEV)

        def one_block(items):
            video_block, video_tag, imu_block, imu_tag, audio_block, audio_tag = items
            loss_imu, video_imu, imu_term = pair_tile(video_block, video_tag, imu_block, imu_tag, scale_imu, offset_imu)
            loss_audio, video_audio, audio_term = pair_tile(video_block, video_tag, audio_block, audio_tag, scale_audio, offset_audio)
            return loss_imu + loss_audio, video_imu + video_audio, imu_term, audio_term

        losses, video_terms, imu_terms, audio_terms = lax.map(one_block, (video_flat, video_tags, imu_now, imu_tag_now, audio_now, audio_tag_now))
        loss_sum = loss_sum + losses
        video_acc = video_acc + video_terms
        imu_acc = imu_acc + jnp.roll(imu_terms.reshape(shape_four), -rotation, axis=0)
        audio_acc = audio_acc + jnp.roll(audio_terms.reshape(shape_four), -rotation, axis=1)
    row_loss = (loss_sum / (2.0 * STEPS * TOK_DEV)).reshape(-1)
    return video_acc.reshape(-1, D), imu_acc.reshape(-1, D), audio_acc.reshape(-1, D), row_loss
```

```python
import functools

import jax
import jax.numpy as jnp
from jax import lax
from jax.experimental import pallas as pl
from jax.experimental.pallas import tpu as pltpu
from jax.sharding import PartitionSpec as P

MESH = pl.DeviceIdType.MESH
STEPS = 4
CHUNKS = 3
LANES = 128
TILE = 64

AUDIO, VIDEO_COL, IMU, VIDEO_ROW = range(4)
STREAMS = (AUDIO, VIDEO_COL, IMU, VIDEO_ROW)
MEETS = {AUDIO: VIDEO_COL, VIDEO_COL: AUDIO, IMU: VIDEO_COL, VIDEO_ROW: IMU}
MEETS_IDS = {AUDIO: 0, VIDEO_COL: 2, IMU: 0, VIDEO_ROW: 1}


def kernel(
    n_row,
    n_col,
    video_hbm,
    imu_hbm,
    audio_hbm,
    video_ids,
    imu_ids,
    audio_ids,
    imu_log_scale,
    imu_bias,
    audio_log_scale,
    audio_bias,
    video_grad,
    imu_grad,
    audio_grad,
    row_loss,
    blocks,
    ids,
    columns,
    grads,
    logits,
    weighted,
    losses,
    send_sem,
    recv_sem,
    id_send_sem,
    id_recv_sem,
    load_sem,
    store_sem,
):
    r, c = lax.axis_index("row"), lax.axis_index("col")
    rows = video_hbm.shape[0]
    width = video_hbm.shape[1]
    piece = rows // CHUNKS

    def away(stream, by):
        if stream == AUDIO:
            return (r, lax.rem(c + by + n_col, n_col))
        if stream == VIDEO_COL:
            return (r, lax.rem(c - by + n_col, n_col))
        if stream == IMU:
            return (lax.rem(r + by + n_row, n_row), c)
        return (lax.rem(r - by + n_row, n_row), c)

    own = {AUDIO: audio_hbm, VIDEO_COL: video_hbm, IMU: imu_hbm, VIDEO_ROW: video_hbm}
    own_ids = {AUDIO: audio_ids, VIDEO_COL: video_ids, IMU: imu_ids, VIDEO_ROW: video_ids}

    def travel(stream, slot, k, source):
        return pltpu.make_async_remote_copy(
            src_ref=source,
            dst_ref=blocks.at[stream, slot, pl.ds(k * piece, piece)],
            send_sem=send_sem.at[stream, slot - 1, k],
            recv_sem=recv_sem.at[stream, slot - 1, k],
            device_id=away(stream, 1),
            device_id_type=MESH,
        )

    def travel_ids(stream, slot):
        return pltpu.make_async_remote_copy(
            src_ref=own_ids[stream],
            dst_ref=ids.at[stream, slot],
            send_sem=id_send_sem.at[stream, slot - 1],
            recv_sem=id_recv_sem.at[stream, slot - 1],
            device_id=away(stream, slot),
            device_id_type=MESH,
        )

    barrier = pltpu.get_barrier_semaphore()
    for stream in STREAMS:
        for by in range(1, STEPS):
            pl.semaphore_signal(barrier, inc=1, device_id=away(stream, by), device_id_type=MESH)

    loads = [
        pltpu.make_async_copy(own[stream], blocks.at[stream, 0], load_sem.at[stream])
        for stream in (AUDIO, VIDEO_COL, IMU)
    ]
    for load in loads:
        load.start()

    pl.semaphore_wait(barrier, len(STREAMS) * (STEPS - 1))

    for k in range(CHUNKS):
        for stream in STREAMS:
            travel(stream, 1, k, own[stream].at[pl.ds(k * piece, piece)]).start()
        if k == 0:
            for stream in STREAMS:
                for slot in range(1, STEPS):
                    travel_ids(stream, slot).start()

    groups = rows // LANES
    for entry, ref in enumerate((video_ids, imu_ids, audio_ids)):
        for g in range(groups):
            across = jnp.broadcast_to(ref[g : g + 1, :], (LANES, LANES))
            columns[entry, g * LANES : (g + 1) * LANES, :] = across.T
    for stream in STREAMS:
        ids[stream, 0] = own_ids[stream][...]
    grads[...] = jnp.zeros_like(grads)
    losses[...] = jnp.zeros_like(losses)

    scales = {
        AUDIO: jnp.exp(jnp.full((1, LANES), audio_log_scale[0])),
        IMU: jnp.exp(jnp.full((1, LANES), imu_log_scale[0])),
    }
    offsets = {AUDIO: audio_bias[0], IMU: imu_bias[0]}
    scales[VIDEO_COL], scales[VIDEO_ROW] = scales[AUDIO], scales[IMU]
    offsets[VIDEO_COL], offsets[VIDEO_ROW] = offsets[AUDIO], offsets[IMU]

    def own_block(stream):
        return blocks.at[VIDEO_COL if stream == VIDEO_ROW else stream, 0]

    def meet(stream, partner, first_group, n_groups):
        mine = own_block(MEETS[stream])
        column = columns.at[MEETS_IDS[stream]]
        with_loss = stream in (AUDIO, IMU)
        scale, offset = scales[stream], offsets[stream]
        partner_ids, partner_rows = partner
        span = n_groups * LANES
        logits[:, :span] = lax.dot_general(
            mine[...], partner_rows[...], (((1,), (1,)), ((), ())), preferred_element_type=jnp.float32
        )

        def tile(t, carry):
            at = pl.ds(pl.multiple_of(t * TILE, TILE), TILE)
            tags = column[at, :]
            total = losses[at, :] if with_loss else None
            for g in range(n_groups):
                lanes = slice(g * LANES, (g + 1) * LANES)
                same = tags == partner_ids[pl.ds(first_group + g, 1), :]
                logit = scale * logits[at, lanes] + offset
                z = jnp.where(same, -logit, logit)
                e = jnp.exp(-jnp.abs(z))
                part = 1.0 / (1.0 + e)
                sigmoid = jnp.where(z >= 0.0, part, e * part)
                weighted[at, lanes] = (jnp.where(same, -sigmoid, sigmoid) * scale).astype(jnp.bfloat16)
                if with_loss:
                    total = total + (jnp.maximum(z, 0.0) + jnp.log1p(e))
            if with_loss:
                losses[at, :] = total
            return carry

        lax.fori_loop(0, rows // TILE, tile, 0)
        step = 256
        for n in range(width // step):
            there = slice(n * step, (n + 1) * step)
            grads[stream, :, there] += jnp.dot(
                weighted[:, :span], partner_rows[:, there], preferred_element_type=jnp.float32
            )

    for load in loads:
        load.wait()

    def whole(slot, carry):
        @pl.when(slot > 0)
        def _():
            for k in range(CHUNKS):
                for stream in STREAMS:
                    here = blocks.at[stream, slot, pl.ds(k * piece, piece)]
                    travel(stream, slot, k, here).wait_recv()
                    travel(stream, slot + 1, k, here).start()
            for stream in STREAMS:
                travel_ids_slot(stream, slot).wait_recv()

        for stream in STREAMS:
            source = blocks.at[stream, slot]
            if stream == VIDEO_ROW:
                source = blocks.at[jnp.where(slot == 0, VIDEO_COL, VIDEO_ROW), slot]
            meet(stream, (ids.at[stream, slot], source), 0, groups)
        return carry

    def travel_ids_slot(stream, slot):
        return pltpu.make_async_remote_copy(
            src_ref=own_ids[stream],
            dst_ref=ids.at[stream, slot],
            send_sem=id_send_sem.at[stream, slot - 1],
            recv_sem=id_recv_sem.at[stream, slot - 1],
            device_id=away(stream, 1),
            device_id_type=MESH,
        )

    lax.fori_loop(0, STEPS - 1, whole, 0)

    last = STEPS - 1
    for stream in STREAMS:
        travel_ids(stream, last).wait_recv()

    def pieces(k, carry):
        for stream in (IMU, VIDEO_ROW, AUDIO, VIDEO_COL):
            here = blocks.at[stream, last, pl.ds(k * piece, piece)]
            travel(stream, last, k, here).wait_recv()
            meet(stream, (ids.at[stream, last], here), k * (piece // LANES), piece // LANES)
        return carry

    lax.fori_loop(0, CHUNKS, pieces, 0)

    stores = [
        pltpu.make_async_copy(grads.at[VIDEO_ROW], imu_grad, store_sem.at[0]),
        pltpu.make_async_copy(grads.at[VIDEO_COL], audio_grad, store_sem.at[1]),
        pltpu.make_async_copy(grads.at[AUDIO], video_grad, store_sem.at[2]),
    ]
    stores[0].start()
    stores[1].start()
    grads[AUDIO] += grads[IMU]
    stores[2].start()
    for g in range(groups):
        across = losses[g * LANES : (g + 1) * LANES, :].T
        row_loss[g : g + 1, :] = jnp.sum(across, axis=0, keepdims=True) / (2.0 * STEPS * rows)
    for store in stores:
        store.wait()

    for stream in STREAMS:
        for slot in range(1, STEPS):
            travel_ids(stream, slot).wait_send()
            for k in range(CHUNKS):
                travel(stream, slot, k, blocks.at[stream, slot, pl.ds(k * piece, piece)]).wait_send()


def per_device(n_row, n_col, *args):
    video_rows, video_ids, imu_rows, imu_ids, audio_rows, audio_ids, *scalars = args
    rows, width = video_rows.shape
    groups = rows // LANES
    as_rows = [tags.reshape(groups, LANES) for tags in (video_ids, imu_ids, audio_ids)]
    grad = jax.ShapeDtypeStruct((rows, width), jnp.float32)
    anywhere = pl.BlockSpec(memory_space=pl.ANY)
    vmem = pl.BlockSpec(memory_space=pltpu.VMEM)
    smem = pl.BlockSpec(memory_space=pltpu.SMEM)
    *grads, row_loss = pl.pallas_call(
        functools.partial(kernel, n_row, n_col),
        out_shape=(grad, grad, grad, jax.ShapeDtypeStruct((groups, LANES), jnp.float32)),
        in_specs=[anywhere] * 3 + [vmem] * 3 + [smem] * 4,
        out_specs=(anywhere, anywhere, anywhere, vmem),
        scratch_shapes=[
            pltpu.VMEM((len(STREAMS), STEPS, rows, width), jnp.bfloat16),
            pltpu.VMEM((len(STREAMS), STEPS, groups, LANES), jnp.int32),
            pltpu.VMEM((3, rows, LANES), jnp.int32),
            pltpu.VMEM((len(STREAMS), rows, width), jnp.float32),
            pltpu.VMEM((rows, rows), jnp.float32),
            pltpu.VMEM((rows, rows), jnp.bfloat16),
            pltpu.VMEM((rows, LANES), jnp.float32),
            pltpu.SemaphoreType.DMA((len(STREAMS), STEPS - 1, CHUNKS)),
            pltpu.SemaphoreType.DMA((len(STREAMS), STEPS - 1, CHUNKS)),
            pltpu.SemaphoreType.DMA((len(STREAMS), STEPS - 1)),
            pltpu.SemaphoreType.DMA((len(STREAMS), STEPS - 1)),
            pltpu.SemaphoreType.DMA((3,)),
            pltpu.SemaphoreType.DMA((3,)),
        ],
        compiler_params=pltpu.CompilerParams(
            collective_id=0, has_side_effects=True, vmem_limit_bytes=52 << 20
        ),
    )(video_rows, imu_rows, audio_rows, *as_rows, *scalars)
    return (*grads, row_loss.reshape(rows))


def solution(mesh):
    spread = P(("row", "col"), None)
    flat = P(("row", "col"))
    return jax.shard_map(
        functools.partial(per_device, mesh.shape["row"], mesh.shape["col"]),
        mesh=mesh,
        in_specs=(spread, flat, spread, flat, spread, flat, P(), P(), P(), P()),
        out_specs=(spread, spread, spread, flat),
        check_vma=False,
    )
```

```python
import functools

import jax
import jax.numpy as jnp
from jax import lax
from jax.experimental import pallas as pl
from jax.experimental.pallas import tpu as pltpu
from jax.sharding import PartitionSpec as P

MESH = pl.DeviceIdType.MESH
STEPS = 4
CHUNKS = 3
LANES = 128
TILE = 64
UNROLL = 6
WIDE = 256

AUDIO, VIDEO_COL, IMU, VIDEO_ROW = range(4)
STREAMS = (AUDIO, VIDEO_COL, IMU, VIDEO_ROW)
OWN_VIDEO, OWN_IMU, OWN_AUDIO = range(3)


def kernel(
    n_row,
    n_col,
    video_hbm,
    imu_hbm,
    audio_hbm,
    video_ids,
    imu_ids,
    audio_ids,
    numbers_hbm,
    video_grad,
    imu_grad,
    audio_grad,
    losses,
    own,
    partners,
    videos,
    relay,
    own_ids,
    ids,
    columns,
    logits,
    weighted,
    numbers,
    send_sem,
    recv_sem,
    relay_send_sem,
    relay_recv_sem,
    id_send_sem,
    id_recv_sem,
    load_sem,
    pair_load_sem,
    id_load_sem,
    number_sem,
):
    r, c = lax.axis_index("row"), lax.axis_index("col")
    rows, width = video_hbm.shape
    piece = rows // CHUNKS
    half = n_row // 2
    place_row, place_col = lax.rem(r, half), lax.rem(c, n_col // 2)
    far = n_col // 2 - 1
    edge = jnp.logical_or(place_col == 0, place_col == far)
    near = jnp.logical_or(place_col == 1, place_col == far - 1)
    inward = c + jnp.where(place_col == 0, 1, -1)
    outward = c + jnp.where(place_col == 1, -1, 1)
    both = jnp.logical_and

    def along_row(by):
        return lax.rem(r + by + n_row, n_row)

    def away(stream, by):
        if stream == AUDIO:
            return (r, lax.rem(c + by + n_col, n_col))
        if stream == VIDEO_COL:
            return (r, lax.rem(c - by + n_col, n_col))
        return (along_row(by if stream == IMU else -by), c)

    source_block = {AUDIO: audio_hbm, VIDEO_COL: video_hbm, IMU: imu_hbm, VIDEO_ROW: video_hbm}
    source_ids = {AUDIO: audio_ids, VIDEO_COL: video_ids, IMU: imu_ids, VIDEO_ROW: video_ids}

    def at(k, size=piece):
        return pl.ds(pl.multiple_of(k * size, size), size)

    def landing(stream, slot, k):
        if stream == AUDIO:
            return partners.at[slot, at(2 * k)]
        if stream == IMU:
            return partners.at[slot, at(2 * k + 1)]
        return videos.at[0 if stream == VIDEO_COL else 1, slot - 1, at(k)]

    def remote(source, target, send, recv, device):
        return pltpu.make_async_remote_copy(
            src_ref=source, dst_ref=target, send_sem=send, recv_sem=recv, device_id=device, device_id_type=MESH
        )

    def travel(stream, slot, k, source):
        return remote(
            source,
            landing(stream, slot, k),
            send_sem.at[stream, slot - 1, k],
            recv_sem.at[stream, slot - 1, k],
            away(stream, 1),
        )

    def passes(stream, slot):
        if stream in (AUDIO, VIDEO_COL):
            return None
        at_wrap = place_row == (half - 1 if stream == IMU else 0)
        elsewhere = jnp.logical_or(slot == 3, both(slot == 2, edge))
        return jnp.logical_not(both(at_wrap, elsewhere))

    def when(condition, action):
        if condition is None:
            action()
        else:
            pl.when(condition)(action)

    def travel_ids(stream, slot, by):
        return remote(
            source_ids[stream],
            ids.at[stream, slot],
            id_send_sem.at[stream, slot - 1],
            id_recv_sem.at[stream, slot - 1],
            away(stream, by),
        )

    def relay_copy(leg, source, buffer, k, device):
        return remote(source, relay.at[buffer, at(k)], relay_send_sem.at[leg, k], relay_recv_sem.at[buffer, k], device)

    def relay_last(leg, buffer, stream, slot, k, device):
        return remote(
            relay.at[buffer, at(k)],
            landing(stream, slot, k),
            relay_send_sem.at[leg, k],
            recv_sem.at[stream, slot - 1, k],
            device,
        )

    over = (along_row(half), c)
    third, second = half - 3, half - 2
    leg_0 = (
        (place_row == third, lambda k: relay_copy(0, imu_hbm.at[at(k)], 0, k, over)),
        (place_row == 2, lambda k: relay_copy(0, video_hbm.at[at(k)], 0, k, over)),
        (both(place_row == second, edge), lambda k: relay_copy(2, imu_hbm.at[at(k)], 1, k, (r, inward))),
        (both(place_row == 1, edge), lambda k: relay_copy(2, video_hbm.at[at(k)], 1, k, (r, inward))),
    )
    leg_1 = (
        (place_row == third, lambda k: relay_last(1, 0, IMU, 3, k, (along_row(-third), c))),
        (place_row == 2, lambda k: relay_last(1, 0, VIDEO_ROW, 3, k, (along_row(third), c))),
    )
    leg_1z = (
        (both(jnp.logical_or(place_row == second, place_row == 1), near), lambda k: relay_copy(3, relay.at[1, at(k)], 2, k, over)),
    )
    leg_2z = (
        (both(place_row == second, near), lambda k: relay_last(4, 2, IMU, 2, k, (along_row(-second), outward))),
        (both(place_row == 1, near), lambda k: relay_last(4, 2, VIDEO_ROW, 2, k, (along_row(second), outward))),
    )

    def relay_arrived(buffer, k):
        return remote(relay.at[buffer, at(k)], relay.at[buffer, at(k)], relay_send_sem.at[0, k], relay_recv_sem.at[buffer, k], over)

    barrier = pltpu.get_barrier_semaphore()

    def greet(*device):
        pl.semaphore_signal(barrier, inc=1, device_id=device, device_id_type=MESH)

    for stream in STREAMS:
        for by in range(1, STEPS):
            greet(*away(stream, by))
    count = len(STREAMS) * (STEPS - 1)
    for condition, devices in (
        (place_row == third, (over, (along_row(-third), c))),
        (place_row == 2, (over, (along_row(third), c))),
        (place_row == 0, ((along_row(third), c),)),
        (place_row == half - 1, ((along_row(-third), c),)),
        (both(place_row == second, near), (over, (along_row(-second), outward))),
        (both(place_row == 1, near), (over, (along_row(second), outward))),
        (both(place_row == 0, edge), ((along_row(second), inward),)),
        (both(place_row == half - 1, edge), ((along_row(-second), inward),)),
    ):

        @pl.when(condition)
        def _(devices=devices):
            for device in devices:
                greet(*device)

        count = count + jnp.where(condition, len(devices), 0)

    loads = [
        pltpu.make_async_copy(source, own.at[entry], load_sem.at[entry])
        for entry, source in ((OWN_VIDEO, video_hbm), (OWN_IMU, imu_hbm), (OWN_AUDIO, audio_hbm))
    ]
    for j, (stream, source) in enumerate(((AUDIO, audio_hbm), (IMU, imu_hbm))):
        for k in range(CHUNKS):
            loads.append(pltpu.make_async_copy(source.at[at(k)], landing(stream, 0, k), pair_load_sem.at[j, k]))
    id_loads = [
        pltpu.make_async_copy(source, own_ids.at[entry], id_load_sem.at[entry])
        for entry, source in ((OWN_VIDEO, video_ids), (OWN_IMU, imu_ids), (OWN_AUDIO, audio_ids))
    ]
    id_loads.append(pltpu.make_async_copy(numbers_hbm, numbers, number_sem))
    for load in id_loads + loads:
        load.start()

    pl.semaphore_wait(barrier, count)

    for k in range(CHUNKS):
        for stream in STREAMS:
            travel(stream, 1, k, source_block[stream].at[at(k)]).start()
        for condition, copy in leg_0:
            when(condition, lambda copy=copy: copy(k).start())
        if k == 0:
            for stream in STREAMS:
                for slot in range(1, STEPS):
                    travel_ids(stream, slot, slot).start()

    groups = rows // LANES
    for load in id_loads:
        load.wait()
    for entry in range(3):
        for g in range(groups):
            across = jnp.broadcast_to(own_ids[entry, g : g + 1, :], (LANES, LANES))
            columns[entry, g * LANES : (g + 1) * LANES, :] = across.T
    for stream, entry in ((AUDIO, OWN_AUDIO), (IMU, OWN_IMU), (VIDEO_COL, OWN_VIDEO), (VIDEO_ROW, OWN_VIDEO)):
        ids[stream, 0] = own_ids[entry]
    for grad in (video_grad, imu_grad, audio_grad):
        grad[...] = jnp.zeros_like(grad)
    losses[...] = jnp.zeros_like(losses)

    log_scale_imu, offset_imu, log_scale_audio, offset_audio = (
        jnp.broadcast_to(numbers[:, n : n + 1], (1, LANES)) for n in range(4)
    )
    scale_imu, scale_audio = jnp.exp(log_scale_imu), jnp.exp(log_scale_audio)

    def meet(entry, grad, partner_rows, tags, kinds):
        span = len(kinds) * LANES
        logits[:, :span] = lax.dot_general(
            own[entry], partner_rows[...], (((1,), (1,)), ((), ())), preferred_element_type=jnp.float32
        )
        with_loss = entry == OWN_VIDEO

        def tile(t, carry):
            here = at(t, TILE)
            mine = columns[entry, here, :]
            total = losses[here, :] if with_loss else None
            for g, stream in enumerate(kinds):
                lanes = slice(g * LANES, (g + 1) * LANES)
                by_col = stream in (AUDIO, VIDEO_COL)
                scale, offset = (scale_audio, offset_audio) if by_col else (scale_imu, offset_imu)
                same = mine == tags[g]
                logit = scale * logits[here, lanes] + offset
                z = jnp.where(same, -logit, logit)
                e = jnp.exp(-jnp.abs(logit))
                part = 1.0 / (1.0 + e)
                sigmoid = jnp.where(z >= 0.0, part, e * part)
                weighted[here, lanes] = (jnp.where(same, -sigmoid, sigmoid) * scale).astype(jnp.bfloat16)
                if with_loss:
                    total = total + (jnp.maximum(z, 0.0) + jnp.log1p(e))
            if with_loss:
                losses[here, :] = total
            return carry

        lax.fori_loop(0, rows // TILE, tile, 0, unroll=UNROLL)
        for n in range(width // WIDE):
            there = slice(n * WIDE, (n + 1) * WIDE)
            grad[:, there] += jnp.dot(
                weighted[:, :span], partner_rows[:, there], preferred_element_type=jnp.float32
            )

    def tag(stream, slot, k):
        return ids[stream, slot, pl.ds(k, 1), :]

    def meet_video(slot, ks, partner_rows):
        tags = [tag(stream, slot, k) for k in ks for stream in (AUDIO, IMU)]
        meet(OWN_VIDEO, video_grad, partner_rows, tags, (AUDIO, IMU) * len(ks))

    def meet_partner(stream, slot, ks, video_rows):
        tags = [tag(stream, slot, k) for k in ks]
        if stream == VIDEO_COL:
            meet(OWN_AUDIO, audio_grad, video_rows, tags, (stream,) * len(ks))
        else:
            meet(OWN_IMU, imu_grad, video_rows, tags, (stream,) * len(ks))

    for load in loads:
        load.wait()
    every = range(CHUNKS)
    meet_video(0, every, partners.at[0])
    meet_partner(VIDEO_COL, 0, every, own.at[OWN_VIDEO])
    meet_partner(VIDEO_ROW, 0, every, own.at[OWN_VIDEO])

    def middle(slot, carry):
        for k in every:
            for stream in STREAMS:
                travel(stream, slot, k, landing(stream, slot, k)).wait_recv()
                when(
                    passes(stream, slot + 1),
                    lambda stream=stream: travel(stream, slot + 1, k, landing(stream, slot, k)).start(),
                )
            for step, buffer, legs in ((1, 0, leg_1), (1, 1, leg_1z), (2, 2, leg_2z)):
                for condition, copy in legs:

                    @pl.when(both(condition, slot == step))
                    def _(buffer=buffer, copy=copy):
                        relay_arrived(buffer, k).wait_recv()
                        copy(k).start()

        for stream in STREAMS:
            travel_ids(stream, slot, 1).wait_recv()
        meet_video(slot, every, partners.at[slot])
        for stream in (VIDEO_COL, VIDEO_ROW):
            meet_partner(stream, slot, every, videos.at[0 if stream == VIDEO_COL else 1, slot - 1])
        return carry

    lax.fori_loop(1, STEPS - 1, middle, 0)

    last = STEPS - 1
    for stream in STREAMS:
        travel_ids(stream, last, 1).wait_recv()

    def pieces(k, carry):
        travel(VIDEO_ROW, last, k, landing(VIDEO_ROW, last, k)).wait_recv()
        meet_partner(VIDEO_ROW, last, (k,), landing(VIDEO_ROW, last, k))
        for stream in (IMU, AUDIO):
            travel(stream, last, k, landing(stream, last, k)).wait_recv()
        meet_video(last, (k,), partners.at[last, at(k, 2 * piece)])
        travel(VIDEO_COL, last, k, landing(VIDEO_COL, last, k)).wait_recv()
        meet_partner(VIDEO_COL, last, (k,), landing(VIDEO_COL, last, k))
        return carry

    lax.fori_loop(0, CHUNKS, pieces, 0)

    for stream in STREAMS:
        for slot in range(1, STEPS):
            travel_ids(stream, slot, slot).wait_send()
            for k in range(CHUNKS):
                when(
                    passes(stream, slot),
                    lambda k=k: travel(stream, slot, k, landing(stream, slot, k)).wait_send(),
                )
    for condition, copy in leg_0 + leg_1 + leg_1z + leg_2z:

        @pl.when(condition)
        def _(copy=copy):
            for k in range(CHUNKS):
                copy(k).wait_send()


def write_out(
    pairs, video_in, imu_in, audio_in, losses, video_out, imu_out, audio_out, loss_out, row_loss, store_sem, loss_sem
):
    stores = [
        pltpu.make_async_copy(source, target, store_sem.at[n])
        for n, (source, target) in enumerate(((video_in, video_out), (imu_in, imu_out), (audio_in, audio_out)))
    ]
    for store in stores:
        store.start()
    for g in range(losses.shape[0] // LANES):
        across = losses[g * LANES : (g + 1) * LANES, :].T
        row_loss[g : g + 1, :] = jnp.sum(across, axis=0, keepdims=True) / pairs
    store = pltpu.make_async_copy(row_loss, loss_out, loss_sem)
    store.start()
    for store in stores + [store]:
        store.wait()


def per_device(n_row, n_col, *args):
    video_rows, video_ids, imu_rows, imu_ids, audio_rows, audio_ids, *scalars = args
    rows, width = video_rows.shape
    groups = rows // LANES
    as_rows = [tags.reshape(groups, LANES) for tags in (video_ids, imu_ids, audio_ids)]
    numbers = jnp.concatenate(scalars).reshape(1, len(scalars))
    operands = (video_rows, imu_rows, audio_rows, *as_rows, numbers)
    grad = jax.ShapeDtypeStruct((rows, width), jnp.float32)
    hbm = pl.BlockSpec(memory_space=pltpu.HBM)
    vmem = pl.BlockSpec(memory_space=pltpu.VMEM)
    dma = pltpu.SemaphoreType.DMA
    sums = pl.pallas_call(
        functools.partial(kernel, n_row, n_col),
        out_shape=(grad, grad, grad, jax.ShapeDtypeStruct((rows, LANES), jnp.float32)),
        in_specs=[hbm] * 7,
        out_specs=(vmem,) * 4,
        scratch_shapes=[
            pltpu.VMEM((3, rows, width), jnp.bfloat16),
            pltpu.VMEM((STEPS, 2 * rows, width), jnp.bfloat16),
            pltpu.VMEM((2, STEPS - 1, rows, width), jnp.bfloat16),
            pltpu.VMEM((3, rows, width), jnp.bfloat16),
            pltpu.VMEM((3, groups, LANES), jnp.int32),
            pltpu.VMEM((len(STREAMS), STEPS, groups, LANES), jnp.int32),
            pltpu.VMEM((3, rows, LANES), jnp.int32),
            pltpu.VMEM((rows, 2 * rows), jnp.float32),
            pltpu.VMEM((rows, 2 * rows), jnp.bfloat16),
            pltpu.VMEM((1, 4), jnp.float32),
            dma((len(STREAMS), STEPS - 1, CHUNKS)),
            dma((len(STREAMS), STEPS - 1, CHUNKS)),
            dma((5, CHUNKS)),
            dma((3, CHUNKS)),
            dma((len(STREAMS), STEPS - 1)),
            dma((len(STREAMS), STEPS - 1)),
            dma((3,)),
            dma((2, CHUNKS)),
            dma((3,)),
            dma,
        ],
        compiler_params=pltpu.CompilerParams(
            collective_id=0, has_side_effects=True, vmem_limit_bytes=40 << 20
        ),
    )(*(pltpu.with_memory_space_constraint(operand, pltpu.HBM) for operand in operands))
    *grads, row_loss = pl.pallas_call(
        functools.partial(write_out, 2.0 * STEPS * rows),
        out_shape=(grad, grad, grad, jax.ShapeDtypeStruct((groups, LANES), jnp.float32)),
        in_specs=[vmem] * 4,
        out_specs=(hbm,) * 4,
        scratch_shapes=[pltpu.VMEM((groups, LANES), jnp.float32), dma((3,)), dma],
        compiler_params=pltpu.CompilerParams(vmem_limit_bytes=4 << 20),
    )(*sums)
    return (*grads, row_loss.reshape(rows))


def solution(mesh):
    spread = P(("row", "col"), None)
    flat = P(("row", "col"))
    return jax.shard_map(
        functools.partial(per_device, mesh.shape["row"], mesh.shape["col"]),
        mesh=mesh,
        in_specs=(spread, flat, spread, flat, spread, flat, P(), P(), P(), P()),
        out_specs=(spread, spread, spread, flat),
        check_vma=False,
    )
```

```python
import functools

import jax
import jax.numpy as jnp
from jax import lax
from jax.experimental import pallas as pl
from jax.experimental.pallas import tpu as pltpu
from jax.sharding import PartitionSpec as P

MESH = pl.DeviceIdType.MESH
STEPS = 4
CHUNKS = 3
LANES = 128
TILE = 64
UNROLL = 6
WIDE = 256

AUDIO, VIDEO_COL, IMU, VIDEO_ROW = range(4)
STREAMS = (AUDIO, VIDEO_COL, IMU, VIDEO_ROW)
ORDER = (AUDIO, VIDEO_COL, IMU, VIDEO_ROW)
START_Z1, START_Z2, START_Y = 0, 2, 4
OWN_VIDEO, OWN_IMU, OWN_AUDIO = range(3)


def kernel(
    n_row,
    n_col,
    video_hbm,
    imu_hbm,
    audio_hbm,
    video_ids,
    imu_ids,
    audio_ids,
    numbers_hbm,
    video_grad,
    imu_grad,
    audio_grad,
    losses,
    own,
    partners,
    videos,
    relay,
    own_ids,
    ids,
    columns,
    logits,
    weighted,
    numbers,
    send_sem,
    recv_sem,
    relay_send_sem,
    relay_recv_sem,
    id_send_sem,
    id_recv_sem,
    load_sem,
    pair_load_sem,
    id_load_sem,
    number_sem,
):
    r, c = lax.axis_index("row"), lax.axis_index("col")
    rows, width = video_hbm.shape
    piece = rows // CHUNKS
    half = n_row // 2
    place_row, place_col = lax.rem(r, half), lax.rem(c, n_col // 2)
    far = n_col // 2 - 1
    edge = jnp.logical_or(place_col == 0, place_col == far)
    near = jnp.logical_or(place_col == 1, place_col == far - 1)
    inward = c + jnp.where(place_col == 0, 1, -1)
    outward = c + jnp.where(place_col == 1, -1, 1)
    both = jnp.logical_and

    def along_row(by):
        return lax.rem(r + by + n_row, n_row)

    def away(stream, by):
        if stream == AUDIO:
            return (r, lax.rem(c + by + n_col, n_col))
        if stream == VIDEO_COL:
            return (r, lax.rem(c - by + n_col, n_col))
        return (along_row(by if stream == IMU else -by), c)

    source_block = {AUDIO: audio_hbm, VIDEO_COL: video_hbm, IMU: imu_hbm, VIDEO_ROW: video_hbm}
    source_ids = {AUDIO: audio_ids, VIDEO_COL: video_ids, IMU: imu_ids, VIDEO_ROW: video_ids}

    def at(k, size=piece):
        return pl.ds(pl.multiple_of(k * size, size), size)

    def landing(stream, slot, k):
        if stream == AUDIO:
            return partners.at[slot, at(2 * k)]
        if stream == IMU:
            return partners.at[slot, at(2 * k + 1)]
        return videos.at[0 if stream == VIDEO_COL else 1, slot - 1, at(k)]

    def remote(source, target, send, recv, device):
        return pltpu.make_async_remote_copy(
            src_ref=source, dst_ref=target, send_sem=send, recv_sem=recv, device_id=device, device_id_type=MESH
        )

    def travel(stream, slot, k, source):
        return remote(
            source,
            landing(stream, slot, k),
            send_sem.at[stream, slot - 1, k],
            recv_sem.at[stream, slot - 1, k],
            away(stream, 1),
        )

    def passes(stream, slot):
        if stream in (AUDIO, VIDEO_COL):
            return None
        at_wrap = place_row == (half - 1 if stream == IMU else 0)
        elsewhere = jnp.logical_or(slot == 3, both(slot == 2, edge))
        return jnp.logical_not(both(at_wrap, elsewhere))

    def when(condition, action):
        if condition is None:
            action()
        else:
            pl.when(condition)(action)

    def travel_ids(stream, slot, by):
        return remote(
            source_ids[stream],
            ids.at[stream, slot],
            id_send_sem.at[stream, slot - 1],
            id_recv_sem.at[stream, slot - 1],
            away(stream, by),
        )

    def relay_copy(leg, source, buffer, k, device):
        return remote(source, relay.at[buffer, at(k)], relay_send_sem.at[leg, k], relay_recv_sem.at[buffer, k], device)

    def relay_last(leg, buffer, stream, slot, k, device):
        return remote(
            relay.at[buffer, at(k)],
            landing(stream, slot, k),
            relay_send_sem.at[leg, k],
            recv_sem.at[stream, slot - 1, k],
            device,
        )

    over = (along_row(half), c)
    third, second = half - 3, half - 2
    leg_0 = (
        (place_row == third, lambda k: relay_copy(0, imu_hbm.at[at(k)], 0, k, over)),
        (place_row == 2, lambda k: relay_copy(0, video_hbm.at[at(k)], 0, k, over)),
        (both(place_row == second, edge), lambda k: relay_copy(2, imu_hbm.at[at(k)], 1, k, (r, inward))),
        (both(place_row == 1, edge), lambda k: relay_copy(2, video_hbm.at[at(k)], 1, k, (r, inward))),
    )
    leg_1 = (
        (place_row == third, lambda k: relay_last(1, 0, IMU, 3, k, (along_row(-third), c))),
        (place_row == 2, lambda k: relay_last(1, 0, VIDEO_ROW, 3, k, (along_row(third), c))),
    )
    leg_1z = (
        (both(jnp.logical_or(place_row == second, place_row == 1), near), lambda k: relay_copy(3, relay.at[1, at(k)], 2, k, over)),
    )
    leg_2z = (
        (both(place_row == second, near), lambda k: relay_last(4, 2, IMU, 2, k, (along_row(-second), outward))),
        (both(place_row == 1, near), lambda k: relay_last(4, 2, VIDEO_ROW, 2, k, (along_row(second), outward))),
    )

    def relay_arrived(buffer, k):
        return remote(relay.at[buffer, at(k)], relay.at[buffer, at(k)], relay_send_sem.at[0, k], relay_recv_sem.at[buffer, k], over)

    barrier = pltpu.get_barrier_semaphore()

    def greet(*device):
        pl.semaphore_signal(barrier, inc=1, device_id=device, device_id_type=MESH)

    for stream in STREAMS:
        for by in range(1, STEPS):
            greet(*away(stream, by))
    count = len(STREAMS) * (STEPS - 1)
    for condition, devices in (
        (place_row == third, (over, (along_row(-third), c))),
        (place_row == 2, (over, (along_row(third), c))),
        (place_row == 0, ((along_row(third), c),)),
        (place_row == half - 1, ((along_row(-third), c),)),
        (both(place_row == second, near), (over, (along_row(-second), outward))),
        (both(place_row == 1, near), (over, (along_row(second), outward))),
        (both(place_row == 0, edge), ((along_row(second), inward),)),
        (both(place_row == half - 1, edge), ((along_row(-second), inward),)),
    ):

        @pl.when(condition)
        def _(devices=devices):
            for device in devices:
                greet(*device)

        count = count + jnp.where(condition, len(devices), 0)

    loads = [
        pltpu.make_async_copy(source, own.at[entry], load_sem.at[entry])
        for entry, source in ((OWN_VIDEO, video_hbm), (OWN_IMU, imu_hbm), (OWN_AUDIO, audio_hbm))
    ]
    for j, (stream, source) in enumerate(((AUDIO, audio_hbm), (IMU, imu_hbm))):
        for k in range(CHUNKS):
            loads.append(pltpu.make_async_copy(source.at[at(k)], landing(stream, 0, k), pair_load_sem.at[j, k]))
    id_loads = [
        pltpu.make_async_copy(source, own_ids.at[entry], id_load_sem.at[entry])
        for entry, source in ((OWN_VIDEO, video_ids), (OWN_IMU, imu_ids), (OWN_AUDIO, audio_ids))
    ]
    id_loads.append(pltpu.make_async_copy(numbers_hbm, numbers, number_sem))
    for load in id_loads + loads:
        load.start()

    pl.semaphore_wait(barrier, count)

    for k in range(CHUNKS):
        for stream in (IMU, VIDEO_ROW):
            travel(stream, 1, k, source_block[stream].at[at(k)]).start()
    for k in range(CHUNKS):
        for stream in (AUDIO, VIDEO_COL):
            travel(stream, 1, k, source_block[stream].at[at(k)]).start()
        for condition, copy in leg_0:
            when(condition, lambda copy=copy: copy(k).start())
        if k == 0:
            for stream in STREAMS:
                for slot in range(1, STEPS):
                    travel_ids(stream, slot, slot).start()

    groups = rows // LANES
    for load in id_loads:
        load.wait()
    for entry in range(3):
        for g in range(groups):
            across = jnp.broadcast_to(own_ids[entry, g : g + 1, :], (LANES, LANES))
            columns[entry, g * LANES : (g + 1) * LANES, :] = across.T
    for stream, entry in ((AUDIO, OWN_AUDIO), (IMU, OWN_IMU), (VIDEO_COL, OWN_VIDEO), (VIDEO_ROW, OWN_VIDEO)):
        ids[stream, 0] = own_ids[entry]
    for grad in (video_grad, imu_grad, audio_grad):
        grad[...] = jnp.zeros_like(grad)
    losses[...] = jnp.zeros_like(losses)

    log_scale_imu, offset_imu, log_scale_audio, offset_audio = (
        jnp.broadcast_to(numbers[:, n : n + 1], (1, LANES)) for n in range(4)
    )
    scale_imu, scale_audio = jnp.exp(log_scale_imu), jnp.exp(log_scale_audio)

    def meet(entry, grad, partner_rows, tags, kinds):
        span = len(kinds) * LANES
        logits[:, :span] = lax.dot_general(
            own[entry], partner_rows[...], (((1,), (1,)), ((), ())), preferred_element_type=jnp.float32
        )
        with_loss = entry == OWN_VIDEO

        def tile(t, carry):
            here = at(t, TILE)
            mine = columns[entry, here, :]
            total = losses[here, :] if with_loss else None
            for g, stream in enumerate(kinds):
                lanes = slice(g * LANES, (g + 1) * LANES)
                by_col = stream in (AUDIO, VIDEO_COL)
                scale, offset = (scale_audio, offset_audio) if by_col else (scale_imu, offset_imu)
                same = mine == tags[g]
                logit = scale * logits[here, lanes] + offset
                z = jnp.where(same, -logit, logit)
                e = jnp.exp(-jnp.abs(logit))
                part = 1.0 / (1.0 + e)
                sigmoid = jnp.where(z >= 0.0, part, e * part)
                weighted[here, lanes] = (jnp.where(same, -sigmoid, sigmoid) * scale).astype(jnp.bfloat16)
                if with_loss:
                    total = total + (jnp.maximum(z, 0.0) + jnp.log1p(e))
            if with_loss:
                losses[here, :] = total
            return carry

        lax.fori_loop(0, rows // TILE, tile, 0, unroll=UNROLL)
        for n in range(width // WIDE):
            there = slice(n * WIDE, (n + 1) * WIDE)
            grad[:, there] += jnp.dot(
                weighted[:, :span], partner_rows[:, there], preferred_element_type=jnp.float32
            )

    def tag(stream, slot, k):
        return ids[stream, slot, pl.ds(k, 1), :]

    def meet_video(slot, ks, partner_rows):
        tags = [tag(stream, slot, k) for k in ks for stream in (AUDIO, IMU)]
        meet(OWN_VIDEO, video_grad, partner_rows, tags, (AUDIO, IMU) * len(ks))

    def meet_partner(stream, slot, ks, video_rows):
        tags = [tag(stream, slot, k) for k in ks]
        if stream == VIDEO_COL:
            meet(OWN_AUDIO, audio_grad, video_rows, tags, (stream,) * len(ks))
        else:
            meet(OWN_IMU, imu_grad, video_rows, tags, (stream,) * len(ks))

    for load in loads:
        load.wait()
    every = range(CHUNKS)
    meet_video(0, every, partners.at[0])
    meet_partner(VIDEO_COL, 0, every, own.at[OWN_VIDEO])
    meet_partner(VIDEO_ROW, 0, every, own.at[OWN_VIDEO])

    def step(t, carry):
        slot, k = 1 + t // CHUNKS, lax.rem(t, CHUNKS)
        for stream in ORDER:
            travel(stream, slot, k, landing(stream, slot, k)).wait_recv()
            onward = slot < STEPS - 1
            allowed = passes(stream, slot + 1)
            pl.when(onward if allowed is None else both(onward, allowed))(
                lambda stream=stream: travel(stream, slot + 1, k, landing(stream, slot, k)).start()
            )
        for start, buffer, legs in ((START_Y, 0, leg_1), (START_Z1, 1, leg_1z), (START_Z2, 2, leg_2z)):
            for condition, copy in legs:

                @pl.when(both(condition, both(t >= start, t < start + CHUNKS)))
                def _(start=start, buffer=buffer, copy=copy):
                    relay_arrived(buffer, t - start).wait_recv()
                    copy(t - start).start()

        @pl.when(k == 0)
        def _():
            for stream in STREAMS:
                travel_ids(stream, slot, 1).wait_recv()

        meet_video(slot, (k,), partners.at[slot, at(k, 2 * piece)])
        meet_partner(VIDEO_COL, slot, (k,), landing(VIDEO_COL, slot, k))
        meet_partner(VIDEO_ROW, slot, (k,), landing(VIDEO_ROW, slot, k))
        return carry

    lax.fori_loop(0, CHUNKS * (STEPS - 1), step, 0)

    for stream in STREAMS:
        for slot in range(1, STEPS):
            travel_ids(stream, slot, slot).wait_send()
            for k in range(CHUNKS):
                when(
                    passes(stream, slot),
                    lambda k=k: travel(stream, slot, k, landing(stream, slot, k)).wait_send(),
                )
    for condition, copy in leg_0 + leg_1 + leg_1z + leg_2z:

        @pl.when(condition)
        def _(copy=copy):
            for k in range(CHUNKS):
                copy(k).wait_send()


def write_out(
    pairs, video_in, imu_in, audio_in, losses, video_out, imu_out, audio_out, loss_out, row_loss, store_sem, loss_sem
):
    stores = [
        pltpu.make_async_copy(source, target, store_sem.at[n])
        for n, (source, target) in enumerate(((video_in, video_out), (imu_in, imu_out), (audio_in, audio_out)))
    ]
    for store in stores:
        store.start()
    for g in range(losses.shape[0] // LANES):
        across = losses[g * LANES : (g + 1) * LANES, :].T
        row_loss[g : g + 1, :] = jnp.sum(across, axis=0, keepdims=True) / pairs
    store = pltpu.make_async_copy(row_loss, loss_out, loss_sem)
    store.start()
    for store in stores + [store]:
        store.wait()


def per_device(n_row, n_col, *args):
    video_rows, video_ids, imu_rows, imu_ids, audio_rows, audio_ids, *scalars = args
    rows, width = video_rows.shape
    groups = rows // LANES
    as_rows = [tags.reshape(groups, LANES) for tags in (video_ids, imu_ids, audio_ids)]
    numbers = jnp.concatenate(scalars).reshape(1, len(scalars))
    operands = (video_rows, imu_rows, audio_rows, *as_rows, numbers)
    grad = jax.ShapeDtypeStruct((rows, width), jnp.float32)
    hbm = pl.BlockSpec(memory_space=pltpu.HBM)
    vmem = pl.BlockSpec(memory_space=pltpu.VMEM)
    dma = pltpu.SemaphoreType.DMA
    sums = pl.pallas_call(
        functools.partial(kernel, n_row, n_col),
        out_shape=(grad, grad, grad, jax.ShapeDtypeStruct((rows, LANES), jnp.float32)),
        in_specs=[hbm] * 7,
        out_specs=(vmem,) * 4,
        scratch_shapes=[
            pltpu.VMEM((3, rows, width), jnp.bfloat16),
            pltpu.VMEM((STEPS, 2 * rows, width), jnp.bfloat16),
            pltpu.VMEM((2, STEPS - 1, rows, width), jnp.bfloat16),
            pltpu.VMEM((3, rows, width), jnp.bfloat16),
            pltpu.VMEM((3, groups, LANES), jnp.int32),
            pltpu.VMEM((len(STREAMS), STEPS, groups, LANES), jnp.int32),
            pltpu.VMEM((3, rows, LANES), jnp.int32),
            pltpu.VMEM((rows, 2 * rows), jnp.float32),
            pltpu.VMEM((rows, 2 * rows), jnp.bfloat16),
            pltpu.VMEM((1, 4), jnp.float32),
            dma((len(STREAMS), STEPS - 1, CHUNKS)),
            dma((len(STREAMS), STEPS - 1, CHUNKS)),
            dma((5, CHUNKS)),
            dma((3, CHUNKS)),
            dma((len(STREAMS), STEPS - 1)),
            dma((len(STREAMS), STEPS - 1)),
            dma((3,)),
            dma((2, CHUNKS)),
            dma((3,)),
            dma,
        ],
        compiler_params=pltpu.CompilerParams(
            collective_id=0, has_side_effects=True, vmem_limit_bytes=40 << 20
        ),
    )(*(pltpu.with_memory_space_constraint(operand, pltpu.HBM) for operand in operands))
    *grads, row_loss = pl.pallas_call(
        functools.partial(write_out, 2.0 * STEPS * rows),
        out_shape=(grad, grad, grad, jax.ShapeDtypeStruct((groups, LANES), jnp.float32)),
        in_specs=[vmem] * 4,
        out_specs=(hbm,) * 4,
        scratch_shapes=[pltpu.VMEM((groups, LANES), jnp.float32), dma((3,)), dma],
        compiler_params=pltpu.CompilerParams(vmem_limit_bytes=4 << 20),
    )(*sums)
    return (*grads, row_loss.reshape(rows))


def solution(mesh):
    spread = P(("row", "col"), None)
    flat = P(("row", "col"))
    return jax.shard_map(
        functools.partial(per_device, mesh.shape["row"], mesh.shape["col"]),
        mesh=mesh,
        in_specs=(spread, flat, spread, flat, spread, flat, P(), P(), P(), P()),
        out_specs=(spread, spread, spread, flat),
        check_vma=False,
    )
```

```python
import functools

import jax
import jax.numpy as jnp
from jax import lax
from jax.experimental import pallas as pl
from jax.experimental.pallas import tpu as pltpu
from jax.sharding import PartitionSpec as P

MESH = pl.DeviceIdType.MESH
STEPS = 4
CHUNKS = 3
LANES = 128
TILE = 64
UNROLL = 6
WIDE = 256

AUDIO, VIDEO_COL, IMU, VIDEO_ROW = range(4)
STREAMS = (AUDIO, VIDEO_COL, IMU, VIDEO_ROW)
ORDER = (AUDIO, VIDEO_COL, IMU, VIDEO_ROW)
START_Z1, START_Z2, START_Y = 0, 2, 4
OWN_VIDEO, OWN_IMU, OWN_AUDIO = range(3)


def kernel(
    n_row,
    n_col,
    video_hbm,
    imu_hbm,
    audio_hbm,
    video_ids,
    imu_ids,
    audio_ids,
    numbers_hbm,
    video_grad,
    imu_grad,
    audio_grad,
    losses,
    own,
    partners,
    videos,
    relay,
    own_ids,
    ids,
    columns,
    logits,
    weighted,
    numbers,
    send_sem,
    recv_sem,
    relay_send_sem,
    relay_recv_sem,
    id_send_sem,
    id_recv_sem,
    load_sem,
    pair_load_sem,
    id_load_sem,
    number_sem,
):
    r, c = lax.axis_index("row"), lax.axis_index("col")
    rows, width = video_hbm.shape
    piece = rows // CHUNKS
    half = n_row // 2
    place_row, place_col = lax.rem(r, half), lax.rem(c, n_col // 2)
    far = n_col // 2 - 1
    edge = jnp.logical_or(place_col == 0, place_col == far)
    near = jnp.logical_or(place_col == 1, place_col == far - 1)
    inward = c + jnp.where(place_col == 0, 1, -1)
    outward = c + jnp.where(place_col == 1, -1, 1)
    both = jnp.logical_and

    def along_row(by):
        return lax.rem(r + by + n_row, n_row)

    def away(stream, by):
        if stream == AUDIO:
            return (r, lax.rem(c + by + n_col, n_col))
        if stream == VIDEO_COL:
            return (r, lax.rem(c - by + n_col, n_col))
        return (along_row(by if stream == IMU else -by), c)

    source_block = {AUDIO: audio_hbm, VIDEO_COL: video_hbm, IMU: imu_hbm, VIDEO_ROW: video_hbm}
    source_ids = {AUDIO: audio_ids, VIDEO_COL: video_ids, IMU: imu_ids, VIDEO_ROW: video_ids}

    def at(k, size=piece):
        return pl.ds(pl.multiple_of(k * size, size), size)

    def landing(stream, slot, k):
        if stream == AUDIO:
            return partners.at[slot, at(2 * k)]
        if stream == IMU:
            return partners.at[slot, at(2 * k + 1)]
        return videos.at[0 if stream == VIDEO_COL else 1, slot - 1, at(k)]

    def remote(source, target, send, recv, device):
        return pltpu.make_async_remote_copy(
            src_ref=source, dst_ref=target, send_sem=send, recv_sem=recv, device_id=device, device_id_type=MESH
        )

    def travel(stream, slot, k, source):
        return remote(
            source,
            landing(stream, slot, k),
            send_sem.at[stream, slot - 1, k],
            recv_sem.at[stream, slot - 1, k],
            away(stream, 1),
        )

    def passes(stream, slot):
        if stream in (AUDIO, VIDEO_COL):
            return None
        at_wrap = place_row == (half - 1 if stream == IMU else 0)
        elsewhere = jnp.logical_or(slot == 3, both(slot == 2, edge))
        return jnp.logical_not(both(at_wrap, elsewhere))

    def when(condition, action):
        if condition is None:
            action()
        else:
            pl.when(condition)(action)

    def travel_ids(stream, slot, by):
        return remote(
            source_ids[stream],
            ids.at[stream, slot],
            id_send_sem.at[stream, slot - 1],
            id_recv_sem.at[stream, slot - 1],
            away(stream, by),
        )

    def relay_copy(leg, source, buffer, k, device):
        return remote(source, relay.at[buffer, at(k)], relay_send_sem.at[leg, k], relay_recv_sem.at[buffer, k], device)

    def relay_last(leg, buffer, stream, slot, k, device):
        return remote(
            relay.at[buffer, at(k)],
            landing(stream, slot, k),
            relay_send_sem.at[leg, k],
            recv_sem.at[stream, slot - 1, k],
            device,
        )

    over = (along_row(half), c)
    third, second = half - 3, half - 2
    leg_0 = (
        (place_row == third, lambda k: relay_copy(0, imu_hbm.at[at(k)], 0, k, over)),
        (place_row == 2, lambda k: relay_copy(0, video_hbm.at[at(k)], 0, k, over)),
        (both(place_row == second, edge), lambda k: relay_copy(2, imu_hbm.at[at(k)], 1, k, (r, inward))),
        (both(place_row == 1, edge), lambda k: relay_copy(2, video_hbm.at[at(k)], 1, k, (r, inward))),
    )
    leg_1 = (
        (place_row == third, lambda k: relay_last(1, 0, IMU, 3, k, (along_row(-third), c))),
        (place_row == 2, lambda k: relay_last(1, 0, VIDEO_ROW, 3, k, (along_row(third), c))),
    )
    leg_1z = (
        (both(jnp.logical_or(place_row == second, place_row == 1), near), lambda k: relay_copy(3, relay.at[1, at(k)], 2, k, over)),
    )
    leg_2z = (
        (both(place_row == second, near), lambda k: relay_last(4, 2, IMU, 2, k, (along_row(-second), outward))),
        (both(place_row == 1, near), lambda k: relay_last(4, 2, VIDEO_ROW, 2, k, (along_row(second), outward))),
    )

    def relay_arrived(buffer, k):
        return remote(relay.at[buffer, at(k)], relay.at[buffer, at(k)], relay_send_sem.at[0, k], relay_recv_sem.at[buffer, k], over)

    barrier = pltpu.get_barrier_semaphore()

    def greet(*device):
        pl.semaphore_signal(barrier, inc=1, device_id=device, device_id_type=MESH)

    for stream in STREAMS:
        for by in range(1, STEPS):
            greet(*away(stream, by))
    count = len(STREAMS) * (STEPS - 1)
    for condition, devices in (
        (place_row == third, (over, (along_row(-third), c))),
        (place_row == 2, (over, (along_row(third), c))),
        (place_row == 0, ((along_row(third), c),)),
        (place_row == half - 1, ((along_row(-third), c),)),
        (both(place_row == second, near), (over, (along_row(-second), outward))),
        (both(place_row == 1, near), (over, (along_row(second), outward))),
        (both(place_row == 0, edge), ((along_row(second), inward),)),
        (both(place_row == half - 1, edge), ((along_row(-second), inward),)),
    ):

        @pl.when(condition)
        def _(devices=devices):
            for device in devices:
                greet(*device)

        count = count + jnp.where(condition, len(devices), 0)

    loads = [
        pltpu.make_async_copy(source, own.at[entry], load_sem.at[entry])
        for entry, source in ((OWN_VIDEO, video_hbm), (OWN_IMU, imu_hbm), (OWN_AUDIO, audio_hbm))
    ]
    for j, (stream, source) in enumerate(((AUDIO, audio_hbm), (IMU, imu_hbm))):
        for k in range(CHUNKS):
            loads.append(pltpu.make_async_copy(source.at[at(k)], landing(stream, 0, k), pair_load_sem.at[j, k]))
    id_loads = [
        pltpu.make_async_copy(source, own_ids.at[entry], id_load_sem.at[entry])
        for entry, source in ((OWN_VIDEO, video_ids), (OWN_IMU, imu_ids), (OWN_AUDIO, audio_ids))
    ]
    id_loads.append(pltpu.make_async_copy(numbers_hbm, numbers, number_sem))
    for load in id_loads + loads:
        load.start()

    pl.semaphore_wait(barrier, count)

    for k in range(CHUNKS):
        for stream in (IMU, VIDEO_ROW):
            travel(stream, 1, k, source_block[stream].at[at(k)]).start()
        for condition, copy in leg_0:
            when(condition, lambda copy=copy: copy(k).start())
    for k in range(CHUNKS):
        for stream in (AUDIO, VIDEO_COL):
            travel(stream, 1, k, source_block[stream].at[at(k)]).start()
        if k == 0:
            for stream in STREAMS:
                for slot in range(1, STEPS):
                    travel_ids(stream, slot, slot).start()

    groups = rows // LANES
    for load in id_loads:
        load.wait()
    for entry in range(3):
        for g in range(groups):
            across = jnp.broadcast_to(own_ids[entry, g : g + 1, :], (LANES, LANES))
            columns[entry, g * LANES : (g + 1) * LANES, :] = across.T
    for stream, entry in ((AUDIO, OWN_AUDIO), (IMU, OWN_IMU), (VIDEO_COL, OWN_VIDEO), (VIDEO_ROW, OWN_VIDEO)):
        ids[stream, 0] = own_ids[entry]
    for grad in (video_grad, imu_grad, audio_grad):
        grad[...] = jnp.zeros_like(grad)
    losses[...] = jnp.zeros_like(losses)

    log_scale_imu, offset_imu, log_scale_audio, offset_audio = (
        jnp.broadcast_to(numbers[:, n : n + 1], (1, LANES)) for n in range(4)
    )
    scale_imu, scale_audio = jnp.exp(log_scale_imu), jnp.exp(log_scale_audio)

    def meet(entry, grad, partner_rows, tags, kinds):
        span = len(kinds) * LANES
        logits[:, :span] = lax.dot_general(
            own[entry], partner_rows[...], (((1,), (1,)), ((), ())), preferred_element_type=jnp.float32
        )
        with_loss = entry == OWN_VIDEO

        def tile(t, carry):
            here = at(t, TILE)
            mine = columns[entry, here, :]
            total = losses[here, :] if with_loss else None
            for g, stream in enumerate(kinds):
                lanes = slice(g * LANES, (g + 1) * LANES)
                by_col = stream in (AUDIO, VIDEO_COL)
                scale, offset = (scale_audio, offset_audio) if by_col else (scale_imu, offset_imu)
                same = mine == tags[g]
                logit = scale * logits[here, lanes] + offset
                z = jnp.where(same, -logit, logit)
                e = jnp.exp(-jnp.abs(logit))
                part = 1.0 / (1.0 + e)
                sigmoid = jnp.where(z >= 0.0, part, e * part)
                weighted[here, lanes] = (jnp.where(same, -sigmoid, sigmoid) * scale).astype(jnp.bfloat16)
                if with_loss:
                    total = total + (jnp.maximum(z, 0.0) + jnp.log1p(e))
            if with_loss:
                losses[here, :] = total
            return carry

        lax.fori_loop(0, rows // TILE, tile, 0, unroll=UNROLL)
        for n in range(width // WIDE):
            there = slice(n * WIDE, (n + 1) * WIDE)
            grad[:, there] += jnp.dot(
                weighted[:, :span], partner_rows[:, there], preferred_element_type=jnp.float32
            )

    def tag(stream, slot, k):
        return ids[stream, slot, pl.ds(k, 1), :]

    def meet_video(slot, ks, partner_rows):
        tags = [tag(stream, slot, k) for k in ks for stream in (AUDIO, IMU)]
        meet(OWN_VIDEO, video_grad, partner_rows, tags, (AUDIO, IMU) * len(ks))

    def meet_partner(stream, slot, ks, video_rows):
        tags = [tag(stream, slot, k) for k in ks]
        if stream == VIDEO_COL:
            meet(OWN_AUDIO, audio_grad, video_rows, tags, (stream,) * len(ks))
        else:
            meet(OWN_IMU, imu_grad, video_rows, tags, (stream,) * len(ks))

    for load in loads:
        load.wait()
    every = range(CHUNKS)
    meet_video(0, every, partners.at[0])
    meet_partner(VIDEO_COL, 0, every, own.at[OWN_VIDEO])
    meet_partner(VIDEO_ROW, 0, every, own.at[OWN_VIDEO])

    def step(t, carry):
        slot, k = 1 + t // CHUNKS, lax.rem(t, CHUNKS)
        for stream in ORDER:
            travel(stream, slot, k, landing(stream, slot, k)).wait_recv()
            onward = slot < STEPS - 1
            allowed = passes(stream, slot + 1)
            pl.when(onward if allowed is None else both(onward, allowed))(
                lambda stream=stream: travel(stream, slot + 1, k, landing(stream, slot, k)).start()
            )
        for start, buffer, legs in ((START_Y, 0, leg_1), (START_Z1, 1, leg_1z), (START_Z2, 2, leg_2z)):
            for condition, copy in legs:

                @pl.when(both(condition, both(t >= start, t < start + CHUNKS)))
                def _(start=start, buffer=buffer, copy=copy):
                    relay_arrived(buffer, t - start).wait_recv()
                    copy(t - start).start()

        @pl.when(k == 0)
        def _():
            for stream in STREAMS:
                travel_ids(stream, slot, 1).wait_recv()

        meet_video(slot, (k,), partners.at[slot, at(k, 2 * piece)])
        meet_partner(VIDEO_COL, slot, (k,), landing(VIDEO_COL, slot, k))
        meet_partner(VIDEO_ROW, slot, (k,), landing(VIDEO_ROW, slot, k))
        return carry

    lax.fori_loop(0, CHUNKS * (STEPS - 1), step, 0)

    for stream in STREAMS:
        for slot in range(1, STEPS):
            travel_ids(stream, slot, slot).wait_send()
            for k in range(CHUNKS):
                when(
                    passes(stream, slot),
                    lambda k=k: travel(stream, slot, k, landing(stream, slot, k)).wait_send(),
                )
    for condition, copy in leg_0 + leg_1 + leg_1z + leg_2z:

        @pl.when(condition)
        def _(copy=copy):
            for k in range(CHUNKS):
                copy(k).wait_send()


def write_out(
    pairs, video_in, imu_in, audio_in, losses, video_out, imu_out, audio_out, loss_out, row_loss, store_sem, loss_sem
):
    stores = [
        pltpu.make_async_copy(source, target, store_sem.at[n])
        for n, (source, target) in enumerate(((video_in, video_out), (imu_in, imu_out), (audio_in, audio_out)))
    ]
    for store in stores:
        store.start()
    for g in range(losses.shape[0] // LANES):
        across = losses[g * LANES : (g + 1) * LANES, :].T
        row_loss[g : g + 1, :] = jnp.sum(across, axis=0, keepdims=True) / pairs
    store = pltpu.make_async_copy(row_loss, loss_out, loss_sem)
    store.start()
    for store in stores + [store]:
        store.wait()


def per_device(n_row, n_col, *args):
    video_rows, video_ids, imu_rows, imu_ids, audio_rows, audio_ids, *scalars = args
    rows, width = video_rows.shape
    groups = rows // LANES
    as_rows = [tags.reshape(groups, LANES) for tags in (video_ids, imu_ids, audio_ids)]
    numbers = jnp.concatenate(scalars).reshape(1, len(scalars))
    operands = (video_rows, imu_rows, audio_rows, *as_rows, numbers)
    grad = jax.ShapeDtypeStruct((rows, width), jnp.float32)
    hbm = pl.BlockSpec(memory_space=pltpu.HBM)
    vmem = pl.BlockSpec(memory_space=pltpu.VMEM)
    dma = pltpu.SemaphoreType.DMA
    sums = pl.pallas_call(
        functools.partial(kernel, n_row, n_col),
        out_shape=(grad, grad, grad, jax.ShapeDtypeStruct((rows, LANES), jnp.float32)),
        in_specs=[hbm] * 7,
        out_specs=(vmem,) * 4,
        scratch_shapes=[
            pltpu.VMEM((3, rows, width), jnp.bfloat16),
            pltpu.VMEM((STEPS, 2 * rows, width), jnp.bfloat16),
            pltpu.VMEM((2, STEPS - 1, rows, width), jnp.bfloat16),
            pltpu.VMEM((3, rows, width), jnp.bfloat16),
            pltpu.VMEM((3, groups, LANES), jnp.int32),
            pltpu.VMEM((len(STREAMS), STEPS, groups, LANES), jnp.int32),
            pltpu.VMEM((3, rows, LANES), jnp.int32),
            pltpu.VMEM((rows, 2 * rows), jnp.float32),
            pltpu.VMEM((rows, 2 * rows), jnp.bfloat16),
            pltpu.VMEM((1, 4), jnp.float32),
            dma((len(STREAMS), STEPS - 1, CHUNKS)),
            dma((len(STREAMS), STEPS - 1, CHUNKS)),
            dma((5, CHUNKS)),
            dma((3, CHUNKS)),
            dma((len(STREAMS), STEPS - 1)),
            dma((len(STREAMS), STEPS - 1)),
            dma((3,)),
            dma((2, CHUNKS)),
            dma((3,)),
            dma,
        ],
        compiler_params=pltpu.CompilerParams(
            collective_id=0, has_side_effects=True, vmem_limit_bytes=40 << 20
        ),
    )(*(pltpu.with_memory_space_constraint(operand, pltpu.HBM) for operand in operands))
    *grads, row_loss = pl.pallas_call(
        functools.partial(write_out, 2.0 * STEPS * rows),
        out_shape=(grad, grad, grad, jax.ShapeDtypeStruct((groups, LANES), jnp.float32)),
        in_specs=[vmem] * 4,
        out_specs=(hbm,) * 4,
        scratch_shapes=[pltpu.VMEM((groups, LANES), jnp.float32), dma((3,)), dma],
        compiler_params=pltpu.CompilerParams(vmem_limit_bytes=4 << 20),
    )(*sums)
    return (*grads, row_loss.reshape(rows))


def solution(mesh):
    spread = P(("row", "col"), None)
    flat = P(("row", "col"))
    return jax.shard_map(
        functools.partial(per_device, mesh.shape["row"], mesh.shape["col"]),
        mesh=mesh,
        in_specs=(spread, flat, spread, flat, spread, flat, P(), P(), P(), P()),
        out_specs=(spread, spread, spread, flat),
        check_vma=False,
    )
```
